32 devices in a mesh: mem: 8 (over z, y), lon: 4 (over x, core).
Axes of the slice: x: 2, y: 2, z: 4, core: 2. Of those that a mesh axis runs over, the one named last changes fastest.
Arguments:
- ensemble: float32 [1024, 4, 8192], P('mem', None, 'lon'), may hold values from -6 to 6
- flow_number_field: float32 [4, 8192], P(None, 'lon'), may hold values from -0.9 to 0.9
- obs_index: int32 [32, 512], P(('mem', 'lon')), may hold values from 0 to 1023
- obs_count: int32 [32], P(('mem', 'lon')), may hold values from 128 to 512, as said below
- obs_dist: int32 [32, 512], P(('mem', 'lon')), may hold values from 0 to 31
- observed_readings: float32 [32, 512], P(('mem', 'lon')), may hold values from -6 to 6
- obs_prec: float32 [32, 512], P(('mem', 'lon')), may hold values from 0.5 to 4
Outputs:
- analysis: float32 [1024, 4, 8192], P('mem', None, 'lon')
The draws below stay inside these ranges and needn't reach their ends.
Inputs may be any that keep to these rules, and one draw needn't show every extreme that they name: `obs_count`: slots from a patch's count on carry no weight; some patch has exactly 512 live slots.
All inputs are finite; a program needn't handle non-finite values. Where the reference program divides by a largest or mean magnitude, that divisor is 1e-20 or more.
Results may differ from the reference program's by a relative error of at most 0.002.
The reference program's roundings to bfloat16 on the way (of `obs_round`, `weighted`, `first_poly`, `root_step`, `second_poly`, `transform` and `perturb_low`) count: a program that leaves them out, or rounds other values in their place, can miss the bound.
Values sent between devices are 32-bit elements; how exact they have to be, the bound alone decides.
A program may use at most 128 MiB of HBM per device.

```python
import math
import jax
import jax.numpy as jnp
from jax import lax

K = 1024
LEV = 4
SUBDOMAIN_WIDTH = 256
OBS_MAX = 512
COL_DEV = 2048
NCOL = 8192
PATCHES = 32
N_MEM = 8
N_LON = 4


def draw_obs_count(key, part):
    first_key, second_key = jax.random.split(jax.random.fold_in(key, 11))
    counts = jax.random.randint(first_key, (PATCHES,), OBS_MAX // 4, OBS_MAX + 1, dtype=jnp.int32)
    full_patch = jax.random.randint(second_key, (), 0, PATCHES, dtype=jnp.int32)
    counts = jnp.where(jnp.arange(PATCHES, dtype=jnp.int32) == full_patch, OBS_MAX, counts)
    return counts.astype(jnp.int32)


def place_ends(array, key, smallest, top_value):
    longest = array.shape.index(max(array.shape))
    spots = []
    for shift in (0, 1):
        where = [jax.random.randint(jax.random.fold_in(key, axis), (), 0, length) for axis, length in enumerate(array.shape)]
        where[longest] = (where[longest] + shift) % array.shape[longest]
        spots.append(tuple(where))
    return array.at[spots[0]].set(smallest).at[spots[1]].set(top_value)


def block_levels(stream_key, dims, pieces, smallest, high):
    loudness, own = 1.0, jax.random.fold_in(stream_key, 6)
    for dim, blocks in pieces:
        heights = jnp.exp(jax.random.uniform(jax.random.fold_in(own, dim), (blocks,), jnp.float32, smallest / len(pieces), high / len(pieces)))
        loudness = loudness * jnp.repeat(heights, dims[dim] // blocks).reshape([-1 if axis == dim else 1 for axis in range(len(dims))])
    return loudness


def gaussian(key, shape, width, limit, pieces=(), kind=jnp.bfloat16):
    entries = width * jax.random.normal(key, shape, jnp.float32)
    if pieces:
        entries = entries * block_levels(key, shape, pieces, -0.22, 0.18)
    return jnp.clip(entries, -limit, limit).astype(kind)


def setup_inputs(seed: int = 0) -> dict:
    keys = jax.random.split(jax.random.key(seed), 8)
    return {
        "ensemble": gaussian(keys[0], (K, LEV, NCOL), 1.0, 6.0, ((0, 8), (2, 4)), jnp.float32),
        "flow_number_field": jnp.clip(jax.random.uniform(keys[1], (LEV, NCOL), jnp.float32, -0.9, 0.9) * block_levels(keys[1], (LEV, NCOL), ((1, 4),), -0.4, 0.0), -0.9, 0.9),
        "obs_index": place_ends(jax.random.randint(keys[2], (PATCHES, OBS_MAX), 0, LEV * SUBDOMAIN_WIDTH), jax.random.fold_in(keys[2], 1), 0, (LEV * SUBDOMAIN_WIDTH) - 1).astype(jnp.int32),
        "obs_count": draw_obs_count(jax.random.fold_in(keys[7], 71), 0),
        "obs_dist": place_ends(jax.random.randint(keys[4], (PATCHES, OBS_MAX), 0, 32), jax.random.fold_in(keys[4], 1), 0, 31).astype(jnp.int32),
        "observed_readings": gaussian(keys[5], (PATCHES, OBS_MAX), 1.0, 6.0, ((0, 32),), jnp.float32),
        "obs_prec": jnp.clip(jnp.exp(math.log(4.0) - 2.0794415 * jax.random.uniform(keys[6], (PATCHES, OBS_MAX), jnp.float32) ** block_levels(keys[6], (PATCHES, OBS_MAX), ((0, 32),), -0.2, 0.2)), 0.5, 4.0),
    }


highest = lax.Precision.HIGHEST
loc_scale = 12.0

def donor_cell_advance(haloed_subdomain, flow_number_field):
    centre = haloed_subdomain[..., 1:-1]
    western = haloed_subdomain[..., :-2]
    eastern = haloed_subdomain[..., 2:]
    return centre - jnp.maximum(flow_number_field, 0.0) * (centre - western) - jnp.minimum(flow_number_field, 0.0) * (eastern - centre)

def analyse(subdomain_slab, obs_cells, live_count, obs_dist, observed_readings, obs_prec):
    members = subdomain_slab.shape[0]
    flat = subdomain_slab.reshape(members, -1)
    column_mean = lax.optimization_barrier(jnp.mean(flat, axis=0))
    perturb = flat - column_mean
    obs_pert = jnp.take(perturb, obs_cells, axis=1)
    obs_round = obs_pert.astype(jnp.bfloat16)
    slots = jnp.arange(obs_cells.shape[0], dtype=jnp.int32)
    weights = jnp.where(slots < live_count, obs_prec * jnp.exp(-0.5 * (obs_dist.astype(jnp.float32) / loc_scale) ** 2), 0.0)
    weighted = (obs_round.astype(jnp.float32) * weights).astype(jnp.bfloat16)
    innovation = observed_readings - jnp.take(column_mean, obs_cells)
    drive = jnp.dot(obs_pert, weights * innovation, precision=highest)
    identity = jnp.eye(members, dtype=jnp.float32)
    gram = (members - 1.0) * identity + jnp.dot(obs_round.astype(jnp.float32), weighted.astype(jnp.float32).T, precision=highest)
    norm_bound = jnp.max(lax.optimization_barrier(jnp.sum(jnp.abs(gram), axis=1)))
    scaled = gram / norm_bound
    scaled_low = scaled.astype(jnp.bfloat16)
    first_poly = (1.5 * identity - 0.5 * scaled).astype(jnp.bfloat16)
    root_step = jnp.dot(scaled_low.astype(jnp.float32), first_poly.astype(jnp.float32), precision=highest).astype(jnp.bfloat16)
    product = jnp.dot(first_poly.astype(jnp.float32), root_step.astype(jnp.float32), precision=highest)
    second_poly = (1.5 * identity - 0.5 * product).astype(jnp.bfloat16)
    inv_root = jnp.dot(second_poly.astype(jnp.float32), first_poly.astype(jnp.float32), precision=highest)
    mean_weight = jnp.dot(inv_root, jnp.dot(inv_root, drive, precision=highest), precision=highest) / norm_bound
    transform = (mean_weight[:, None] + jnp.sqrt((members - 1.0) / norm_bound) * inv_root).astype(jnp.bfloat16)
    perturb_low = perturb.astype(jnp.bfloat16)
    result = column_mean + jnp.dot(transform.astype(jnp.float32).T, perturb_low.astype(jnp.float32), precision=highest)
    return result.reshape(subdomain_slab.shape)

def reference(ensemble, flow_number_field, obs_index, obs_count, obs_dist, observed_readings, obs_prec):
    haloed_subdomain = jnp.concatenate([ensemble[..., -1:], ensemble, ensemble[..., :1]], axis=2)
    predicted_member_states = donor_cell_advance(haloed_subdomain, flow_number_field)

    def one_patch(patch_id):
        group_id = patch_id // N_LON
        tile_id = patch_id % N_LON
        leading_longitude_offset = (tile_id * COL_DEV + group_id * SUBDOMAIN_WIDTH).astype(jnp.int32)
        subdomain_slab = lax.dynamic_slice_in_dim(predicted_member_states, leading_longitude_offset, SUBDOMAIN_WIDTH, axis=2)
        return analyse(subdomain_slab, obs_index[patch_id], obs_count[patch_id], obs_dist[patch_id], observed_readings[patch_id], obs_prec[patch_id])
    cycle_outputs = lax.map(one_patch, jnp.arange(PATCHES, dtype=jnp.int32))
    cycle_outputs = cycle_outputs.reshape(N_MEM, N_LON, K, LEV, SUBDOMAIN_WIDTH).transpose(2, 3, 1, 0, 4)
    return cycle_outputs.reshape(K, LEV, NCOL)
```

```python
import functools
import jax
import jax.numpy as jnp
from jax import lax
from jax.experimental import pallas as pl
from jax.experimental.pallas import tpu as pltpu
from jax.sharding import PartitionSpec as P

loc_scale = 12.0
MESH = pl.DeviceIdType.MESH
f32, bf16 = jnp.float32, jnp.bfloat16


def forecast(ensemble, flow):
    field = jnp.transpose(ensemble, (1, 0, 2))
    peers = lax.axis_size("lon")
    up = [(i, (i + 1) % peers) for i in range(peers)]
    down = [(j, i) for i, j in up]
    before = lax.ppermute(ensemble[..., -1:], "lon", up)
    after = lax.ppermute(ensemble[..., :1], "lon", down)
    before = jnp.transpose(before, (1, 0, 2))
    after = jnp.transpose(after, (1, 0, 2))
    west = jnp.concatenate([before, field[..., :-1]], axis=2)
    east = jnp.concatenate([field[..., 1:], after], axis=2)
    flow = flow[:, None, :]
    return field - jnp.maximum(flow, 0.0) * (field - west) - jnp.minimum(flow, 0.0) * (east - field)


def dot(a, b, dims):
    return lax.dot_general(a, b, (dims, ((), ())), preferred_element_type=f32)


def three_rows(row):
    hi = row.astype(bf16).astype(f32)
    mid = (row - hi).astype(bf16).astype(f32)
    low = row - hi - mid
    which = lax.broadcasted_iota(jnp.int32, (16, row.shape[1]), 0)
    rows = jnp.where(which == 0, hi, jnp.where(which == 1, mid, jnp.where(which == 2, low, 0.0)))
    return rows.astype(bf16)


def as_row(column):
    wide = jnp.broadcast_to(column, (column.shape[0], 128))
    return wide.T[0:1, :]


def kernel(n, fc, cells, weights, readings, out, slab, low, onehot, obs, wtd, big, poly_a, poly_b,
           poly_c, rows, outbuf, send1, recv1, send2, recv2, local):
    levels, members, width = slab.shape
    group = members // n
    me = lax.axis_index("mem")
    total_cells = levels * width
    step = 256
    blocks = members // step

    barrier = pltpu.get_barrier_semaphore()

    def greet(s, _):
        pl.semaphore_signal(barrier, inc=1, device_id={"mem": lax.rem(me + s, n)}, device_id_type=MESH)
        return 0

    lax.fori_loop(1, n, greet, 0)
    pl.semaphore_wait(barrier, n - 1)

    def there(dst, owner):
        return pltpu.make_async_remote_copy(
            src_ref=fc.at[:, :, pl.ds(pl.multiple_of(dst * width, width), width)],
            dst_ref=slab.at[:, pl.ds(pl.multiple_of(owner * group, group), group), :],
            send_sem=send1.at[dst], recv_sem=recv1.at[owner],
            device_id={"mem": dst}, device_id_type=MESH)

    def back(dst, owner):
        return pltpu.make_async_remote_copy(
            src_ref=outbuf.at[:, pl.ds(pl.multiple_of(dst * group, group), group), :],
            dst_ref=out.at[:, :, pl.ds(pl.multiple_of(owner * width, width), width)],
            send_sem=send2.at[dst], recv_sem=recv2.at[owner],
            device_id={"mem": dst}, device_id_type=MESH)

    def go(s, _):
        there(lax.rem(me + s, n), me).start()
        return 0

    lax.fori_loop(1, n, go, 0)
    mine_rows = pl.ds(pl.multiple_of(me * group, group), group)
    mine_columns = pl.ds(pl.multiple_of(me * width, width), width)
    own = pltpu.make_async_copy(fc.at[:, :, mine_columns], slab.at[:, mine_rows, :], local.at[0])
    own.start()

    def fill(b, _):
        at = pl.ds(pl.multiple_of(b * step, step), step)
        cell = lax.broadcasted_iota(jnp.int32, (step, onehot.shape[1]), 0) + b * step
        onehot[at, :] = jnp.where(cell == cells[...], 1.0, 0.0).astype(bf16)
        return 0

    lax.fori_loop(0, total_cells // step, fill, 0)

    def block_sum(src):
        at = pl.ds(pl.multiple_of(src * group, group), group)
        return jnp.concatenate(
            [jnp.sum(slab[l, at, :], axis=0, keepdims=True) for l in range(levels)], axis=1)

    own.wait()

    def gather(s, acc):
        src = lax.rem(me + n - s, n)
        there(src, src).wait_recv()
        return acc + block_sum(src)

    mean = lax.fori_loop(1, n, gather, block_sum(me)) / members
    rows[0:1, :] = mean

    picked = jnp.sum(dot(three_rows(mean), onehot[...], ((1,), (0,))), axis=0, keepdims=True)
    forcing = weights[...] * (readings[...] - picked)
    coef = jnp.sum(dot(three_rows(forcing), onehot[...], ((1,), (1,))), axis=0, keepdims=True)

    def centre(b, _):
        at = pl.ds(pl.multiple_of(b * step, step), step)
        drive = jnp.zeros((step, width), f32)
        for l in range(levels):
            part = slice(l * width, (l + 1) * width)
            p = slab[l, at, :] - mean[:, part]
            low[at, part] = p.astype(bf16)
            drive = drive + p * coef[:, part]
        rows[1:2, at] = as_row(jnp.sum(drive, axis=1, keepdims=True))
        o = dot(low[at, :], onehot[...], ((1,), (0,)))
        obs[at, :] = o.astype(bf16)
        wtd[at, :] = (o.astype(bf16).astype(f32) * weights[...]).astype(bf16)
        return 0

    lax.fori_loop(0, blocks, centre, 0)

    def eye(b):
        r = lax.broadcasted_iota(jnp.int32, (step, members), 0) + b * step
        return r == lax.broadcasted_iota(jnp.int32, (step, members), 1)

    def make_gram(b, bound):
        at = pl.ds(pl.multiple_of(b * step, step), step)
        g = dot(obs[at, :], wtd[...], ((1,), (1,))) + jnp.where(eye(b), members - 1.0, 0.0)
        big[at, :] = g
        sums = jnp.sum(jnp.abs(g), axis=1, keepdims=True)
        return jnp.maximum(bound, jnp.max(sums, axis=0, keepdims=True))

    bound = lax.fori_loop(0, blocks, make_gram, jnp.zeros((1, 1), f32))

    def first(b, _):
        at = pl.ds(pl.multiple_of(b * step, step), step)
        scaled = big[at, :] / bound
        poly_a[at, :] = scaled.astype(bf16)
        poly_b[at, :] = (jnp.where(eye(b), 1.5, 0.0) - 0.5 * scaled).astype(bf16)
        return 0

    lax.fori_loop(0, blocks, first, 0)

    def root(b, _):
        at = pl.ds(pl.multiple_of(b * step, step), step)
        poly_c[at, :] = dot(poly_a[at, :], poly_b[...], ((1,), (0,))).astype(bf16)
        return 0

    lax.fori_loop(0, blocks, root, 0)

    def second(b, _):
        at = pl.ds(pl.multiple_of(b * step, step), step)
        product = dot(poly_b[at, :], poly_c[...], ((1,), (0,)))
        s = (jnp.where(eye(b), 1.5, 0.0) - 0.5 * product).astype(bf16)
        inv = dot(s, poly_b[...], ((1,), (0,)))
        big[at, :] = inv
        rows[2:3, at] = as_row(jnp.sum(inv * rows[1:2, :], axis=1, keepdims=True))
        return 0

    lax.fori_loop(0, blocks, second, 0)
    stretch = jnp.sqrt((members - 1.0) / bound)

    def transform(b, _):
        at = pl.ds(pl.multiple_of(b * step, step), step)
        inv = big[at, :]
        weight = jnp.sum(inv * rows[2:3, :], axis=1, keepdims=True) / bound
        poly_a[at, :] = (weight + stretch * inv).astype(bf16)
        return 0

    lax.fori_loop(0, blocks, transform, 0)

    tile = max(128, group)
    tiles = members // tile
    each = tile // group

    def apply(t, _):
        b = lax.rem(me // each + 1 + t, tiles)
        at = pl.ds(pl.multiple_of(b * tile, tile), tile)
        value = dot(poly_a[:, at], low[...], ((0,), (0,))) + rows[0:1, :]
        for l in range(levels):
            outbuf[l, at, :] = value[:, l * width:(l + 1) * width]
        for g in range(each):
            dst = b * each + g

            @pl.when(dst != me)
            def _():
                back(dst, me).start()
        return 0

    lax.fori_loop(0, tiles, apply, 0)
    own_out = pltpu.make_async_copy(outbuf.at[:, mine_rows, :], out.at[:, :, mine_columns], local.at[1])
    own_out.start()

    def finish(s, _):
        src = lax.rem(me + n - s, n)
        back(src, src).wait_recv()
        back(src, me).wait_send()
        there(src, me).wait_send()
        return 0

    lax.fori_loop(1, n, finish, 0)
    own_out.wait()


def per_device(ensemble, flow, obs_index, obs_count, obs_dist, readings, prec):
    n = lax.axis_size("mem")
    levels = ensemble.shape[1]
    members = ensemble.shape[0] * n
    columns = ensemble.shape[2]
    width = columns // n
    cells, slots = levels * width, obs_index.shape[1]
    fc = forecast(ensemble, flow)
    live = lax.broadcasted_iota(jnp.int32, (1, slots), 1) < obs_count[0]
    weights = jnp.where(live, prec * jnp.exp(-0.5 * (obs_dist.astype(f32) / loc_scale) ** 2), 0.0)
    vmem = pl.BlockSpec(memory_space=pltpu.VMEM)
    hbm = pl.BlockSpec(memory_space=pl.ANY)
    result = pl.pallas_call(
        functools.partial(kernel, n),
        out_shape=jax.ShapeDtypeStruct(fc.shape, f32),
        in_specs=[hbm, vmem, vmem, vmem],
        out_specs=hbm,
        scratch_shapes=[
            pltpu.VMEM((levels, members, width), f32),
            pltpu.VMEM((members, cells), bf16),
            pltpu.VMEM((cells, slots), bf16),
            pltpu.VMEM((members, slots), bf16),
            pltpu.VMEM((members, slots), bf16),
            pltpu.VMEM((members, members), f32),
            pltpu.VMEM((members, members), bf16),
            pltpu.VMEM((members, members), bf16),
            pltpu.VMEM((members, members), bf16),
            pltpu.VMEM((8, max(members, cells)), f32),
            pltpu.VMEM((levels, members, width), f32),
            pltpu.SemaphoreType.DMA((n,)),
            pltpu.SemaphoreType.DMA((n,)),
            pltpu.SemaphoreType.DMA((n,)),
            pltpu.SemaphoreType.DMA((n,)),
            pltpu.SemaphoreType.DMA((2,)),
        ],
        compiler_params=pltpu.CompilerParams(
            collective_id=0, has_side_effects=True, vmem_limit_bytes=60 * 1024 * 1024),
        name="regroup_analyse",
    )(fc, obs_index, weights, readings)
    return jnp.transpose(result, (1, 0, 2))


def solution(mesh):
    placed = (
        P("mem", None, "lon"),
        P(None, "lon"),
        P(("mem", "lon"), None),
        P(("mem", "lon")),
        P(("mem", "lon"), None),
        P(("mem", "lon"), None),
        P(("mem", "lon"), None),
    )
    return jax.shard_map(
        per_device, mesh=mesh, in_specs=placed, out_specs=P("mem", None, "lon"), check_vma=False
    )
```

```python
import functools
import jax
import jax.numpy as jnp
from jax import lax
from jax.experimental import pallas as pl
from jax.experimental.pallas import tpu as pltpu
from jax.sharding import PartitionSpec as P

loc_scale = 12.0
MESH = pl.DeviceIdType.MESH
f32, bf16 = jnp.float32, jnp.bfloat16


def forecast(ensemble, flow):
    field = jnp.transpose(ensemble, (1, 0, 2))
    peers = lax.axis_size("lon")
    up = [(i, (i + 1) % peers) for i in range(peers)]
    down = [(j, i) for i, j in up]
    before = lax.ppermute(ensemble[..., -1:], "lon", up)
    after = lax.ppermute(ensemble[..., :1], "lon", down)
    before = jnp.transpose(before, (1, 0, 2))
    after = jnp.transpose(after, (1, 0, 2))
    west = jnp.concatenate([before, field[..., :-1]], axis=2)
    east = jnp.concatenate([field[..., 1:], after], axis=2)
    flow = flow[:, None, :]
    return field - jnp.maximum(flow, 0.0) * (field - west) - jnp.minimum(flow, 0.0) * (east - field)


def dot(a, b, dims):
    return lax.dot_general(a, b, (dims, ((), ())), preferred_element_type=f32)


def three_rows(row):
    hi = row.astype(bf16).astype(f32)
    mid = (row - hi).astype(bf16).astype(f32)
    low = row - hi - mid
    which = lax.broadcasted_iota(jnp.int32, (16, row.shape[1]), 0)
    rows = jnp.where(which == 0, hi, jnp.where(which == 1, mid, jnp.where(which == 2, low, 0.0)))
    return rows.astype(bf16)


def as_row(column):
    wide = jnp.broadcast_to(column, (column.shape[0], 128))
    return wide.T[0:1, :]


def kernel(n, fc, cells, weights, readings, out, slab, low, onehot, obs, wtd, big, poly_a, poly_b,
           poly_c, rows, outbuf, send1, recv1, send2, recv2, local, gate):
    levels, members, width = slab.shape
    group = members // n
    me = lax.axis_index("mem")
    total_cells = levels * width
    step = 256
    blocks = members // step

    lon = lax.axis_index("lon")
    paired = lax.axis_size("lon") % 2 == 0
    second_of_pair = lax.rem(lon, 2) == 1
    partner = lon + 1 - 2 * lax.rem(lon, 2)
    barrier = pltpu.get_barrier_semaphore()
    if paired:
        pl.semaphore_signal(barrier, inc=1, device_id={"lon": partner}, device_id_type=MESH)

    def greet(s, _):
        pl.semaphore_signal(barrier, inc=1, device_id={"mem": lax.rem(me + s, n)}, device_id_type=MESH)
        return 0

    lax.fori_loop(1, n, greet, 0)
    pl.semaphore_wait(barrier, n if paired else n - 1)

    def there(dst, owner):
        return pltpu.make_async_remote_copy(
            src_ref=fc.at[:, :, pl.ds(pl.multiple_of(dst * width, width), width)],
            dst_ref=slab.at[:, pl.ds(pl.multiple_of(owner * group, group), group), :],
            send_sem=send1.at[dst], recv_sem=recv1.at[owner],
            device_id={"mem": dst}, device_id_type=MESH)

    def back(dst, owner):
        return pltpu.make_async_remote_copy(
            src_ref=outbuf.at[:, pl.ds(pl.multiple_of(dst * group, group), group), :],
            dst_ref=out.at[:, :, pl.ds(pl.multiple_of(owner * width, width), width)],
            send_sem=send2.at[dst], recv_sem=recv2.at[owner],
            device_id={"mem": dst}, device_id_type=MESH)

    def go(s, _):
        there(lax.rem(me + s, n), me).start()
        return 0

    if paired:

        @pl.when(second_of_pair)
        def _():
            pl.semaphore_wait(gate, 1)

    lax.fori_loop(1, n, go, 0)
    mine_rows = pl.ds(pl.multiple_of(me * group, group), group)
    mine_columns = pl.ds(pl.multiple_of(me * width, width), width)
    own = pltpu.make_async_copy(fc.at[:, :, mine_columns], slab.at[:, mine_rows, :], local.at[0])
    own.start()

    def fill(b, _):
        at = pl.ds(pl.multiple_of(b * step, step), step)
        cell = lax.broadcasted_iota(jnp.int32, (step, onehot.shape[1]), 0) + b * step
        onehot[at, :] = jnp.where(cell == cells[...], 1.0, 0.0).astype(bf16)
        return 0

    lax.fori_loop(0, total_cells // step, fill, 0)

    def sent(s, _):
        there(lax.rem(me + s, n), me).wait_send()
        return 0

    lax.fori_loop(1, n, sent, 0)
    if paired:

        @pl.when(jnp.logical_not(second_of_pair))
        def _():
            pl.semaphore_signal(gate, inc=1, device_id={"lon": partner}, device_id_type=MESH)

    def block_sum(src):
        at = pl.ds(pl.multiple_of(src * group, group), group)
        return jnp.concatenate(
            [jnp.sum(slab[l, at, :], axis=0, keepdims=True) for l in range(levels)], axis=1)

    own.wait()

    def gather(s, acc):
        src = lax.rem(me + n - s, n)
        there(src, src).wait_recv()
        return acc + block_sum(src)

    mean = lax.fori_loop(1, n, gather, block_sum(me)) / members
    rows[0:1, :] = mean

    picked = jnp.sum(dot(three_rows(mean), onehot[...], ((1,), (0,))), axis=0, keepdims=True)
    forcing = weights[...] * (readings[...] - picked)
    coef = jnp.sum(dot(three_rows(forcing), onehot[...], ((1,), (1,))), axis=0, keepdims=True)

    def centre(b, _):
        at = pl.ds(pl.multiple_of(b * step, step), step)
        drive = jnp.zeros((step, width), f32)
        for l in range(levels):
            part = slice(l * width, (l + 1) * width)
            p = slab[l, at, :] - mean[:, part]
            low[at, part] = p.astype(bf16)
            drive = drive + p * coef[:, part]
        rows[1:2, at] = as_row(jnp.sum(drive, axis=1, keepdims=True))
        o = dot(low[at, :], onehot[...], ((1,), (0,)))
        obs[at, :] = o.astype(bf16)
        wtd[at, :] = (o.astype(bf16).astype(f32) * weights[...]).astype(bf16)
        return 0

    lax.fori_loop(0, blocks, centre, 0)

    def eye(b):
        r = lax.broadcasted_iota(jnp.int32, (step, members), 0) + b * step
        return r == lax.broadcasted_iota(jnp.int32, (step, members), 1)

    def make_gram(b, bound):
        at = pl.ds(pl.multiple_of(b * step, step), step)
        g = dot(obs[at, :], wtd[...], ((1,), (1,))) + jnp.where(eye(b), members - 1.0, 0.0)
        big[at, :] = g
        sums = jnp.sum(jnp.abs(g), axis=1, keepdims=True)
        return jnp.maximum(bound, jnp.max(sums, axis=0, keepdims=True))

    bound = lax.fori_loop(0, blocks, make_gram, jnp.zeros((1, 1), f32))

    def first(b, _):
        at = pl.ds(pl.multiple_of(b * step, step), step)
        scaled = big[at, :] / bound
        poly_a[at, :] = scaled.astype(bf16)
        poly_b[at, :] = (jnp.where(eye(b), 1.5, 0.0) - 0.5 * scaled).astype(bf16)
        return 0

    lax.fori_loop(0, blocks, first, 0)

    def root(b, _):
        at = pl.ds(pl.multiple_of(b * step, step), step)
        poly_c[at, :] = dot(poly_a[at, :], poly_b[...], ((1,), (0,))).astype(bf16)
        return 0

    lax.fori_loop(0, blocks, root, 0)

    def second(b, _):
        at = pl.ds(pl.multiple_of(b * step, step), step)
        product = dot(poly_b[at, :], poly_c[...], ((1,), (0,)))
        s = (jnp.where(eye(b), 1.5, 0.0) - 0.5 * product).astype(bf16)
        inv = dot(s, poly_b[...], ((1,), (0,)))
        big[at, :] = inv
        rows[2:3, at] = as_row(jnp.sum(inv * rows[1:2, :], axis=1, keepdims=True))
        return 0

    lax.fori_loop(0, blocks, second, 0)
    stretch = jnp.sqrt((members - 1.0) / bound)

    def transform(b, _):
        at = pl.ds(pl.multiple_of(b * step, step), step)
        inv = big[at, :]
        weight = jnp.sum(inv * rows[2:3, :], axis=1, keepdims=True) / bound
        poly_a[at, :] = (weight + stretch * inv).astype(bf16)
        return 0

    lax.fori_loop(0, blocks, transform, 0)

    tile = max(128, group)
    tiles = members // tile
    each = tile // group

    def apply(t, _):
        b = lax.rem(me // each + 1 + t, tiles)
        at = pl.ds(pl.multiple_of(b * tile, tile), tile)
        value = dot(poly_a[:, at], low[...], ((0,), (0,))) + rows[0:1, :]
        for l in range(levels):
            outbuf[l, at, :] = value[:, l * width:(l + 1) * width]
        for g in range(each):
            dst = b * each + g

            @pl.when(dst != me)
            def _():
                back(dst, me).start()
        return 0

    lax.fori_loop(0, tiles, apply, 0)
    own_out = pltpu.make_async_copy(outbuf.at[:, mine_rows, :], out.at[:, :, mine_columns], local.at[1])
    own_out.start()

    def finish(s, _):
        src = lax.rem(me + n - s, n)
        back(src, src).wait_recv()
        back(src, me).wait_send()
        return 0

    lax.fori_loop(1, n, finish, 0)
    own_out.wait()


def per_device(ensemble, flow, obs_index, obs_count, obs_dist, readings, prec):
    n = lax.axis_size("mem")
    levels = ensemble.shape[1]
    members = ensemble.shape[0] * n
    columns = ensemble.shape[2]
    width = columns // n
    cells, slots = levels * width, obs_index.shape[1]
    fc = forecast(ensemble, flow)
    live = lax.broadcasted_iota(jnp.int32, (1, slots), 1) < obs_count[0]
    weights = jnp.where(live, prec * jnp.exp(-0.5 * (obs_dist.astype(f32) / loc_scale) ** 2), 0.0)
    vmem = pl.BlockSpec(memory_space=pltpu.VMEM)
    hbm = pl.BlockSpec(memory_space=pl.ANY)
    result = pl.pallas_call(
        functools.partial(kernel, n),
        out_shape=jax.ShapeDtypeStruct(fc.shape, f32),
        in_specs=[hbm, vmem, vmem, vmem],
        out_specs=hbm,
        scratch_shapes=[
            pltpu.VMEM((levels, members, width), f32),
            pltpu.VMEM((members, cells), bf16),
            pltpu.VMEM((cells, slots), bf16),
            pltpu.VMEM((members, slots), bf16),
            pltpu.VMEM((members, slots), bf16),
            pltpu.VMEM((members, members), f32),
            pltpu.VMEM((members, members), bf16),
            pltpu.VMEM((members, members), bf16),
            pltpu.VMEM((members, members), bf16),
            pltpu.VMEM((8, max(members, cells)), f32),
            pltpu.VMEM((levels, members, width), f32),
            pltpu.SemaphoreType.DMA((n,)),
            pltpu.SemaphoreType.DMA((n,)),
            pltpu.SemaphoreType.DMA((n,)),
            pltpu.SemaphoreType.DMA((n,)),
            pltpu.SemaphoreType.DMA((2,)),
            pltpu.SemaphoreType.REGULAR,
        ],
        compiler_params=pltpu.CompilerParams(
            collective_id=0, has_side_effects=True, vmem_limit_bytes=60 * 1024 * 1024),
        name="regroup_analyse",
    )(fc, obs_index, weights, readings)
    return jnp.transpose(result, (1, 0, 2))


def solution(mesh):
    placed = (
        P("mem", None, "lon"),
        P(None, "lon"),
        P(("mem", "lon"), None),
        P(("mem", "lon")),
        P(("mem", "lon"), None),
        P(("mem", "lon"), None),
        P(("mem", "lon"), None),
    )
    return jax.shard_map(
        per_device, mesh=mesh, in_specs=placed, out_specs=P("mem", None, "lon"), check_vma=False
    )
```

```python
import functools
import jax
import jax.numpy as jnp
from jax import lax
from jax.experimental import pallas as pl
from jax.experimental.pallas import tpu as pltpu
from jax.sharding import PartitionSpec as P

loc_scale = 12.0
MESH = pl.DeviceIdType.MESH
f32, bf16 = jnp.float32, jnp.bfloat16


def dot(a, b, dims):
    return lax.dot_general(a, b, (dims, ((), ())), preferred_element_type=f32)


def three_rows(row):
    hi = row.astype(bf16).astype(f32)
    mid = (row - hi).astype(bf16).astype(f32)
    low = row - hi - mid
    which = lax.broadcasted_iota(jnp.int32, (16, row.shape[1]), 0)
    rows = jnp.where(which == 0, hi, jnp.where(which == 1, mid, jnp.where(which == 2, low, 0.0)))
    return rows.astype(bf16)


def as_row(column):
    wide = jnp.broadcast_to(column, (column.shape[0], 128))
    return wide.T[0:1, :]


def kernel(n, ens, flow, cells, count, dist, prec, readings, out, field, slab, low, onehot, obs, wtd, big,
           poly_a, poly_b, poly_c, rows, outbuf, backbuf, edges, loads, stores, send1, recv1, send2, recv2,
           local, gate):
    levels, members, width = slab.shape
    group = members // n
    columns = n * width
    pad = 128
    me = lax.axis_index("mem")
    total_cells = levels * width
    step = 256
    blocks = members // step
    lon, peers = lax.axis_index("lon"), lax.axis_size("lon")
    lon_east, lon_west = lax.rem(lon + 1, peers), lax.rem(lon + peers - 1, peers)
    paired = peers % 2 == 0
    second_of_pair = lax.rem(lon, 2) == 1
    partner = lon + 1 - 2 * lax.rem(lon, 2)

    inputs = [pltpu.make_async_copy(ens.at[:, l, :], field.at[l, :, pad:pad + columns], loads.at[l])
              for l in range(levels)]
    for load in inputs:
        load.start()

    barrier = pltpu.get_barrier_semaphore()
    for side in (lon_east, lon_west):
        pl.semaphore_signal(barrier, inc=1, device_id={"lon": side}, device_id_type=MESH)

    def greet(s, _):
        pl.semaphore_signal(barrier, inc=1, device_id={"mem": lax.rem(me + s, n)}, device_id_type=MESH)
        return 0

    lax.fori_loop(1, n, greet, 0)
    pl.semaphore_wait(barrier, n + 1)

    halo = []
    for l in range(levels):
        for side, (dst, take, put) in enumerate((
                (lon_east, columns - pad, 0), (lon_west, 0, pad + columns))):
            halo.append(pltpu.make_async_remote_copy(
                src_ref=ens.at[:, l, take:take + pad], dst_ref=field.at[l, :, put:put + pad],
                send_sem=edges.at[0, side, l], recv_sem=edges.at[1, side, l],
                device_id={"lon": dst}, device_id_type=MESH))
    for edge in halo:
        edge.start()

    def rows_of(device):
        return pl.ds(pl.multiple_of(device * group, group), group)

    def columns_of(device):
        return pl.ds(pl.multiple_of(device * width, width), width)

    def there(dst, owner):
        return pltpu.make_async_remote_copy(
            src_ref=outbuf.at[:, rows_of(dst), :], dst_ref=slab.at[:, rows_of(owner), :],
            send_sem=send1.at[dst], recv_sem=recv1.at[owner],
            device_id={"mem": dst}, device_id_type=MESH)

    def back(dst, owner):
        return pltpu.make_async_remote_copy(
            src_ref=outbuf.at[:, rows_of(dst), :], dst_ref=backbuf.at[:, rows_of(owner), :],
            send_sem=send2.at[dst], recv_sem=recv2.at[owner],
            device_id={"mem": dst}, device_id_type=MESH)

    def place(owner):
        return [pltpu.make_async_copy(
            backbuf.at[l, rows_of(owner), :], out.at[:, l, columns_of(owner)], stores.at[owner, l])
            for l in range(levels)]

    def advance(dst):
        for l in range(levels):
            value = field[l, :, pl.ds(pl.multiple_of(dst * width, 128), width + 2 * pad)]
            span = width + 2 * pad
            west = pltpu.roll(value, 1, 1)[:, pad:pad + width]
            east = pltpu.roll(value, span - 1, 1)[:, pad:pad + width]
            centre = value[:, pad:pad + width]
            f = flow[l:l + 1, columns_of(dst)]
            outbuf[l, rows_of(dst), :] = (
                centre - jnp.maximum(f, 0.0) * (centre - west) - jnp.minimum(f, 0.0) * (east - centre))

    own = pltpu.make_async_copy(outbuf.at[:, rows_of(me), :], slab.at[:, rows_of(me), :], local.at[0])
    for load in inputs:
        load.wait()

    def send_forecast(dst):
        advance(dst)

        @pl.when(dst != me)
        def _():
            there(dst, me).start()

        @pl.when(dst == me)
        def _():
            own.start()

    if paired:

        @pl.when(second_of_pair)
        def _():
            pl.semaphore_wait(gate, 1)

    def inner(s, _):
        send_forecast(1 + lax.rem(me + s, n - 2))
        return 0

    lax.fori_loop(0, n - 2, inner, 0)
    for edge in halo:
        edge.wait()

    def outer(s, _):
        send_forecast(s * (n - 1))
        return 0

    lax.fori_loop(0, 2, outer, 0)

    def fill(b, _):
        at = pl.ds(pl.multiple_of(b * step, step), step)
        cell = lax.broadcasted_iota(jnp.int32, (step, onehot.shape[1]), 0) + b * step
        onehot[at, :] = jnp.where(cell == cells[...], 1.0, 0.0).astype(bf16)
        return 0

    lax.fori_loop(0, total_cells // step, fill, 0)
    live = lax.broadcasted_iota(jnp.int32, cells.shape, 1) < count[...]
    reach = prec[...] * jnp.exp(-0.5 * (dist[...].astype(f32) / loc_scale) ** 2)
    weights = jnp.where(live, reach, 0.0)

    def sent(s, _):
        there(lax.rem(me + s, n), me).wait_send()
        return 0

    lax.fori_loop(1, n, sent, 0)
    if paired:

        @pl.when(jnp.logical_not(second_of_pair))
        def _():
            pl.semaphore_signal(gate, inc=1, device_id={"lon": partner}, device_id_type=MESH)

    def block_sum(src):
        at = pl.ds(pl.multiple_of(src * group, group), group)
        return jnp.concatenate(
            [jnp.sum(slab[l, at, :], axis=0, keepdims=True) for l in range(levels)], axis=1)

    own.wait()

    def gather(s, acc):
        src = lax.rem(me + n - s, n)
        there(src, src).wait_recv()
        return acc + block_sum(src)

    mean = lax.fori_loop(1, n, gather, block_sum(me)) / members
    rows[0:1, :] = mean

    picked = jnp.sum(dot(three_rows(mean), onehot[...], ((1,), (0,))), axis=0, keepdims=True)
    forcing = weights * (readings[...] - picked)
    coef = jnp.sum(dot(three_rows(forcing), onehot[...], ((1,), (1,))), axis=0, keepdims=True)

    def centre(b, _):
        at = pl.ds(pl.multiple_of(b * step, step), step)
        drive = jnp.zeros((step, width), f32)
        for l in range(levels):
            part = slice(l * width, (l + 1) * width)
            p = slab[l, at, :] - mean[:, part]
            low[at, part] = p.astype(bf16)
            drive = drive + p * coef[:, part]
        rows[1:2, at] = as_row(jnp.sum(drive, axis=1, keepdims=True))
        o = dot(low[at, :], onehot[...], ((1,), (0,)))
        obs[at, :] = o.astype(bf16)
        wtd[at, :] = (o.astype(bf16).astype(f32) * weights).astype(bf16)
        return 0

    lax.fori_loop(0, blocks, centre, 0)

    def eye(b):
        r = lax.broadcasted_iota(jnp.int32, (step, members), 0) + b * step
        return r == lax.broadcasted_iota(jnp.int32, (step, members), 1)

    def make_gram(b, bound):
        at = pl.ds(pl.multiple_of(b * step, step), step)
        g = dot(obs[at, :], wtd[...], ((1,), (1,))) + jnp.where(eye(b), members - 1.0, 0.0)
        big[at, :] = g
        sums = jnp.sum(jnp.abs(g), axis=1, keepdims=True)
        return jnp.maximum(bound, jnp.max(sums, axis=0, keepdims=True))

    bound = lax.fori_loop(0, blocks, make_gram, jnp.zeros((1, 1), f32))

    def first(b, _):
        at = pl.ds(pl.multiple_of(b * step, step), step)
        scaled = big[at, :] / bound
        poly_a[at, :] = scaled.astype(bf16)
        poly_b[at, :] = (jnp.where(eye(b), 1.5, 0.0) - 0.5 * scaled).astype(bf16)
        return 0

    lax.fori_loop(0, blocks, first, 0)

    def root(b, _):
        at = pl.ds(pl.multiple_of(b * step, step), step)
        poly_c[at, :] = dot(poly_a[at, :], poly_b[...], ((1,), (0,))).astype(bf16)
        return 0

    lax.fori_loop(0, blocks, root, 0)

    def second(b, _):
        at = pl.ds(pl.multiple_of(b * step, step), step)
        product = dot(poly_b[at, :], poly_c[...], ((1,), (0,)))
        s = (jnp.where(eye(b), 1.5, 0.0) - 0.5 * product).astype(bf16)
        inv = dot(s, poly_b[...], ((1,), (0,)))
        big[at, :] = inv
        rows[2:3, at] = as_row(jnp.sum(inv * rows[1:2, :], axis=1, keepdims=True))
        return 0

    lax.fori_loop(0, blocks, second, 0)
    stretch = jnp.sqrt((members - 1.0) / bound)

    def transform(b, _):
        at = pl.ds(pl.multiple_of(b * step, step), step)
        inv = big[at, :]
        weight = jnp.sum(inv * rows[2:3, :], axis=1, keepdims=True) / bound
        poly_a[at, :] = (weight + stretch * inv).astype(bf16)
        return 0

    lax.fori_loop(0, blocks, transform, 0)

    tile = max(128, group)
    tiles = members // tile
    each = tile // group

    def apply(t, _):
        b = lax.rem(me // each + 1 + t, tiles)
        at = pl.ds(pl.multiple_of(b * tile, tile), tile)
        value = dot(poly_a[:, at], low[...], ((0,), (0,))) + rows[0:1, :]
        for l in range(levels):
            outbuf[l, at, :] = value[:, l * width:(l + 1) * width]
        for g in range(each):
            dst = b * each + g

            @pl.when(dst != me)
            def _():
                back(dst, me).start()
        return 0

    lax.fori_loop(0, tiles, apply, 0)
    backbuf[:, rows_of(me), :] = outbuf[:, rows_of(me), :]
    for put in place(me):
        put.start()

    def arrive(s, _):
        src = lax.rem(me + n - s, n)
        back(src, src).wait_recv()
        for put in place(src):
            put.start()
        return 0

    lax.fori_loop(1, n, arrive, 0)

    def finish(s, _):
        dst = lax.rem(me + n - s, n)
        back(dst, me).wait_send()
        for put in place(dst):
            put.wait()
        return 0

    lax.fori_loop(1, n, finish, 0)
    for put in place(me):
        put.wait()


def per_device(ensemble, flow, obs_index, obs_count, obs_dist, readings, prec):
    n = lax.axis_size("mem")
    group, levels, columns = ensemble.shape
    members, width = group * n, columns // n
    cells, slots = levels * width, obs_index.shape[1]
    vmem = pl.BlockSpec(memory_space=pltpu.VMEM)
    hbm = pl.BlockSpec(memory_space=pl.ANY)
    slab = pltpu.VMEM((levels, members, width), f32)
    square = pltpu.VMEM((members, members), bf16)
    return pl.pallas_call(
        functools.partial(kernel, n),
        out_shape=jax.ShapeDtypeStruct(ensemble.shape, f32),
        in_specs=[hbm] + [vmem] * 6,
        out_specs=hbm,
        scratch_shapes=[
            pltpu.VMEM((levels, group, columns + 256), f32),
            slab,
            pltpu.VMEM((members, cells), bf16),
            pltpu.VMEM((cells, slots), bf16),
            pltpu.VMEM((members, slots), bf16),
            pltpu.VMEM((members, slots), bf16),
            pltpu.VMEM((members, members), f32),
            square,
            square,
            square,
            pltpu.VMEM((8, max(members, cells)), f32),
            slab,
            slab,
            pltpu.SemaphoreType.DMA((2, 2, levels)),
            pltpu.SemaphoreType.DMA((levels,)),
            pltpu.SemaphoreType.DMA((n, levels)),
            pltpu.SemaphoreType.DMA((n,)),
            pltpu.SemaphoreType.DMA((n,)),
            pltpu.SemaphoreType.DMA((n,)),
            pltpu.SemaphoreType.DMA((n,)),
            pltpu.SemaphoreType.DMA((1,)),
            pltpu.SemaphoreType.REGULAR,
        ],
        compiler_params=pltpu.CompilerParams(
            collective_id=0, has_side_effects=True, vmem_limit_bytes=60 * 1024 * 1024),
        name="regroup_analyse",
    )(ensemble, flow, obs_index, obs_count[:, None], obs_dist, prec, readings)


def solution(mesh):
    placed = (
        P("mem", None, "lon"),
        P(None, "lon"),
        P(("mem", "lon"), None),
        P(("mem", "lon")),
        P(("mem", "lon"), None),
        P(("mem", "lon"), None),
        P(("mem", "lon"), None),
    )
    return jax.shard_map(
        per_device, mesh=mesh, in_specs=placed, out_specs=P("mem", None, "lon"), check_vma=False
    )
```

```python
import functools
import jax
import jax.numpy as jnp
from jax import lax
from jax.experimental import pallas as pl
from jax.experimental.pallas import tpu as pltpu
from jax.sharding import PartitionSpec as P

loc_scale = 12.0
MESH = pl.DeviceIdType.MESH
f32, bf16 = jnp.float32, jnp.bfloat16


def dot(a, b, dims):
    return lax.dot_general(a, b, (dims, ((), ())), preferred_element_type=f32)


def three_rows(row):
    hi = row.astype(bf16).astype(f32)
    mid = (row - hi).astype(bf16).astype(f32)
    low = row - hi - mid
    which = lax.broadcasted_iota(jnp.int32, (16, row.shape[1]), 0)
    rows = jnp.where(which == 0, hi, jnp.where(which == 1, mid, jnp.where(which == 2, low, 0.0)))
    return rows.astype(bf16)


def as_row(column):
    wide = jnp.broadcast_to(column, (column.shape[0], 128))
    return wide.T[0:1, :]


def kernel(n, ens, flow, cells, count, dist, prec, readings, out, field, slab, low, onehot, obs, wtd, big,
           poly_a, poly_b, poly_c, rows, outbuf, backbuf, edges, loads, stores, send1, recv1, send2, recv2,
           local, gate):
    levels, members, width = slab.shape
    group = members // n
    columns = n * width
    pad = 128
    me = lax.axis_index("mem")
    total_cells = levels * width
    step = 256
    blocks = members // step
    lon, peers = lax.axis_index("lon"), lax.axis_size("lon")
    lon_east, lon_west = lax.rem(lon + 1, peers), lax.rem(lon + peers - 1, peers)
    paired = peers % 2 == 0
    second_of_pair = lax.rem(lon, 2) == 1
    partner = lon + 1 - 2 * lax.rem(lon, 2)

    inputs = [pltpu.make_async_copy(ens.at[:, l, :], field.at[l, :, pad:pad + columns], loads.at[l])
              for l in range(levels)]
    for load in inputs:
        load.start()

    barrier = pltpu.get_barrier_semaphore()
    for side in (lon_east, lon_west):
        pl.semaphore_signal(barrier, inc=1, device_id={"lon": side}, device_id_type=MESH)

    def greet(s, _):
        pl.semaphore_signal(barrier, inc=1, device_id={"mem": lax.rem(me + s, n)}, device_id_type=MESH)
        return 0

    lax.fori_loop(1, n, greet, 0)
    pl.semaphore_wait(barrier, n + 1)

    halo = []
    for l in range(levels):
        for side, (dst, take, put) in enumerate((
                (lon_east, columns - pad, 0), (lon_west, 0, pad + columns))):
            halo.append(pltpu.make_async_remote_copy(
                src_ref=ens.at[:, l, take:take + pad], dst_ref=field.at[l, :, put:put + pad],
                send_sem=edges.at[0, side, l], recv_sem=edges.at[1, side, l],
                device_id={"lon": dst}, device_id_type=MESH))
    for edge in halo:
        edge.start()

    def rows_of(device):
        return pl.ds(pl.multiple_of(device * group, group), group)

    def columns_of(device):
        return pl.ds(pl.multiple_of(device * width, width), width)

    def there(dst, owner):
        return pltpu.make_async_remote_copy(
            src_ref=outbuf.at[:, rows_of(dst), :], dst_ref=slab.at[:, rows_of(owner), :],
            send_sem=send1.at[dst], recv_sem=recv1.at[owner],
            device_id={"mem": dst}, device_id_type=MESH)

    def back(dst, owner):
        return pltpu.make_async_remote_copy(
            src_ref=outbuf.at[:, rows_of(dst), :], dst_ref=backbuf.at[:, rows_of(owner), :],
            send_sem=send2.at[dst], recv_sem=recv2.at[owner],
            device_id={"mem": dst}, device_id_type=MESH)

    def place(owner):
        return [pltpu.make_async_copy(
            backbuf.at[l, rows_of(owner), :], out.at[:, l, columns_of(owner)], stores.at[owner, l])
            for l in range(levels)]

    def advance(dst):
        for l in range(levels):
            value = field[l, :, pl.ds(pl.multiple_of(dst * width, 128), width + 2 * pad)]
            span = width + 2 * pad
            west = pltpu.roll(value, 1, 1)[:, pad:pad + width]
            east = pltpu.roll(value, span - 1, 1)[:, pad:pad + width]
            centre = value[:, pad:pad + width]
            f = flow[l:l + 1, columns_of(dst)]
            outbuf[l, rows_of(dst), :] = (
                centre - jnp.maximum(f, 0.0) * (centre - west) - jnp.minimum(f, 0.0) * (east - centre))

    def nth(s, mine, count):
        if count % 2:
            return lax.rem(mine + s, count)
        half = count // 2
        upper = mine // half
        outer = ((4 * mine < count) | (4 * mine >= 3 * count)).astype(jnp.int32)
        side = lax.rem(upper + s // half + 1 - outer, 2)
        j = lax.rem(s, half)
        return jnp.where(side == 1, half + j, half - 1 - j)

    own = pltpu.make_async_copy(outbuf.at[:, rows_of(me), :], slab.at[:, rows_of(me), :], local.at[0])
    for load in inputs:
        load.wait()

    def send_forecast(dst):
        advance(dst)

        @pl.when(dst != me)
        def _():
            there(dst, me).start()

        @pl.when(dst == me)
        def _():
            own.start()

    if paired:

        @pl.when(second_of_pair)
        def _():
            pl.semaphore_wait(gate, 1)

    def serve(s, _):
        send_forecast(nth(s, me, n))
        return 0

    early = 0 if n % 2 else n // 2 - 1
    lax.fori_loop(0, early, serve, 0)
    for edge in halo:
        edge.wait()
    lax.fori_loop(early, n, serve, 0)

    def fill(b, _):
        at = pl.ds(pl.multiple_of(b * step, step), step)
        cell = lax.broadcasted_iota(jnp.int32, (step, onehot.shape[1]), 0) + b * step
        onehot[at, :] = jnp.where(cell == cells[...], 1.0, 0.0).astype(bf16)
        return 0

    lax.fori_loop(0, total_cells // step, fill, 0)
    live = lax.broadcasted_iota(jnp.int32, cells.shape, 1) < count[...]
    reach = prec[...] * jnp.exp(-0.5 * (dist[...].astype(f32) / loc_scale) ** 2)
    weights = jnp.where(live, reach, 0.0)

    def sent(s, _):
        there(lax.rem(me + s, n), me).wait_send()
        return 0

    lax.fori_loop(1, n, sent, 0)
    if paired:

        @pl.when(jnp.logical_not(second_of_pair))
        def _():
            pl.semaphore_signal(gate, inc=1, device_id={"lon": partner}, device_id_type=MESH)

    def block_sum(src):
        at = pl.ds(pl.multiple_of(src * group, group), group)
        return jnp.concatenate(
            [jnp.sum(slab[l, at, :], axis=0, keepdims=True) for l in range(levels)], axis=1)

    own.wait()

    def gather(s, acc):
        src = lax.rem(me + n - s, n)
        there(src, src).wait_recv()
        return acc + block_sum(src)

    mean = lax.fori_loop(1, n, gather, block_sum(me)) / members
    rows[0:1, :] = mean

    picked = jnp.sum(dot(three_rows(mean), onehot[...], ((1,), (0,))), axis=0, keepdims=True)
    forcing = weights * (readings[...] - picked)
    coef = jnp.sum(dot(three_rows(forcing), onehot[...], ((1,), (1,))), axis=0, keepdims=True)

    def centre(b, _):
        at = pl.ds(pl.multiple_of(b * step, step), step)
        drive = jnp.zeros((step, width), f32)
        for l in range(levels):
            part = slice(l * width, (l + 1) * width)
            p = slab[l, at, :] - mean[:, part]
            low[at, part] = p.astype(bf16)
            drive = drive + p * coef[:, part]
        rows[1:2, at] = as_row(jnp.sum(drive, axis=1, keepdims=True))
        o = dot(low[at, :], onehot[...], ((1,), (0,)))
        obs[at, :] = o.astype(bf16)
        wtd[at, :] = (o.astype(bf16).astype(f32) * weights).astype(bf16)
        return 0

    lax.fori_loop(0, blocks, centre, 0)

    def eye(b):
        r = lax.broadcasted_iota(jnp.int32, (step, members), 0) + b * step
        return r == lax.broadcasted_iota(jnp.int32, (step, members), 1)

    def make_gram(b, bound):
        at = pl.ds(pl.multiple_of(b * step, step), step)
        g = dot(obs[at, :], wtd[...], ((1,), (1,))) + jnp.where(eye(b), members - 1.0, 0.0)
        big[at, :] = g
        sums = jnp.sum(jnp.abs(g), axis=1, keepdims=True)
        return jnp.maximum(bound, jnp.max(sums, axis=0, keepdims=True))

    bound = lax.fori_loop(0, blocks, make_gram, jnp.zeros((1, 1), f32))

    def first(b, _):
        at = pl.ds(pl.multiple_of(b * step, step), step)
        scaled = big[at, :] / bound
        poly_a[at, :] = scaled.astype(bf16)
        poly_b[at, :] = (jnp.where(eye(b), 1.5, 0.0) - 0.5 * scaled).astype(bf16)
        return 0

    lax.fori_loop(0, blocks, first, 0)

    def root(b, _):
        at = pl.ds(pl.multiple_of(b * step, step), step)
        poly_c[at, :] = dot(poly_a[at, :], poly_b[...], ((1,), (0,))).astype(bf16)
        return 0

    lax.fori_loop(0, blocks, root, 0)

    def second(b, _):
        at = pl.ds(pl.multiple_of(b * step, step), step)
        product = dot(poly_b[at, :], poly_c[...], ((1,), (0,)))
        s = (jnp.where(eye(b), 1.5, 0.0) - 0.5 * product).astype(bf16)
        inv = dot(s, poly_b[...], ((1,), (0,)))
        big[at, :] = inv
        rows[2:3, at] = as_row(jnp.sum(inv * rows[1:2, :], axis=1, keepdims=True))
        return 0

    lax.fori_loop(0, blocks, second, 0)
    stretch = jnp.sqrt((members - 1.0) / bound)

    def transform(b, _):
        at = pl.ds(pl.multiple_of(b * step, step), step)
        inv = big[at, :]
        weight = jnp.sum(inv * rows[2:3, :], axis=1, keepdims=True) / bound
        poly_a[at, :] = (weight + stretch * inv).astype(bf16)
        return 0

    lax.fori_loop(0, blocks, transform, 0)

    tile = max(128, group)
    tiles = members // tile
    each = tile // group

    def apply(t, _):
        b = nth(t, me // each, tiles)
        at = pl.ds(pl.multiple_of(b * tile, tile), tile)
        value = dot(poly_a[:, at], low[...], ((0,), (0,))) + rows[0:1, :]
        for l in range(levels):
            outbuf[l, at, :] = value[:, l * width:(l + 1) * width]
        for g in range(each):
            dst = b * each + g

            @pl.when(dst != me)
            def _():
                back(dst, me).start()
        return 0

    lax.fori_loop(0, tiles, apply, 0)
    backbuf[:, rows_of(me), :] = outbuf[:, rows_of(me), :]
    for put in place(me):
        put.start()

    def arrive(s, _):
        src = lax.rem(me + n - s, n)
        back(src, src).wait_recv()
        for put in place(src):
            put.start()
        return 0

    lax.fori_loop(1, n, arrive, 0)

    def finish(s, _):
        dst = lax.rem(me + n - s, n)
        back(dst, me).wait_send()
        for put in place(dst):
            put.wait()
        return 0

    lax.fori_loop(1, n, finish, 0)
    for put in place(me):
        put.wait()


def per_device(ensemble, flow, obs_index, obs_count, obs_dist, readings, prec):
    n = lax.axis_size("mem")
    group, levels, columns = ensemble.shape
    members, width = group * n, columns // n
    cells, slots = levels * width, obs_index.shape[1]
    vmem = pl.BlockSpec(memory_space=pltpu.VMEM)
    hbm = pl.BlockSpec(memory_space=pl.ANY)
    slab = pltpu.VMEM((levels, members, width), f32)
    square = pltpu.VMEM((members, members), bf16)
    return pl.pallas_call(
        functools.partial(kernel, n),
        out_shape=jax.ShapeDtypeStruct(ensemble.shape, f32),
        in_specs=[hbm] + [vmem] * 6,
        out_specs=hbm,
        scratch_shapes=[
            pltpu.VMEM((levels, group, columns + 256), f32),
            slab,
            pltpu.VMEM((members, cells), bf16),
            pltpu.VMEM((cells, slots), bf16),
            pltpu.VMEM((members, slots), bf16),
            pltpu.VMEM((members, slots), bf16),
            pltpu.VMEM((members, members), f32),
            square,
            square,
            square,
            pltpu.VMEM((8, max(members, cells)), f32),
            slab,
            slab,
            pltpu.SemaphoreType.DMA((2, 2, levels)),
            pltpu.SemaphoreType.DMA((levels,)),
            pltpu.SemaphoreType.DMA((n, levels)),
            pltpu.SemaphoreType.DMA((n,)),
            pltpu.SemaphoreType.DMA((n,)),
            pltpu.SemaphoreType.DMA((n,)),
            pltpu.SemaphoreType.DMA((n,)),
            pltpu.SemaphoreType.DMA((1,)),
            pltpu.SemaphoreType.REGULAR,
        ],
        compiler_params=pltpu.CompilerParams(
            collective_id=0, has_side_effects=True, vmem_limit_bytes=60 * 1024 * 1024),
        name="regroup_analyse",
    )(ensemble, flow, obs_index, obs_count[:, None], obs_dist, prec, readings)


def solution(mesh):
    placed = (
        P("mem", None, "lon"),
        P(None, "lon"),
        P(("mem", "lon"), None),
        P(("mem", "lon")),
        P(("mem", "lon"), None),
        P(("mem", "lon"), None),
        P(("mem", "lon"), None),
    )
    return jax.shard_map(
        per_device, mesh=mesh, in_specs=placed, out_specs=P("mem", None, "lon"), check_vma=False
    )
```

```python
import functools
import jax
import jax.numpy as jnp
from jax import lax
from jax.experimental import pallas as pl
from jax.experimental.pallas import tpu as pltpu
from jax.sharding import PartitionSpec as P

loc_scale = 12.0
MESH = pl.DeviceIdType.MESH
f32, bf16 = jnp.float32, jnp.bfloat16


def dot(a, b, dims):
    return lax.dot_general(a, b, (dims, ((), ())), preferred_element_type=f32)


def three_rows(row):
    hi = row.astype(bf16).astype(f32)
    mid = (row - hi).astype(bf16).astype(f32)
    low = row - hi - mid
    which = lax.broadcasted_iota(jnp.int32, (16, row.shape[1]), 0)
    rows = jnp.where(which == 0, hi, jnp.where(which == 1, mid, jnp.where(which == 2, low, 0.0)))
    return rows.astype(bf16)


def as_row(column):
    wide = jnp.broadcast_to(column, (column.shape[0], 128))
    return wide.T[0:1, :]


def kernel(n, ens, flow, cells, count, dist, prec, readings, out, field, slab, low, onehot, obs, wtd, big,
           poly_a, poly_b, poly_c, rows, outbuf, backbuf, edges, loads, stores, send1, recv1, send2, recv2,
           local, gate):
    levels, members, width = slab.shape
    group = members // n
    columns = n * width
    pad = 128
    me = lax.axis_index("mem")
    total_cells = levels * width
    step = 256
    blocks = members // step
    lon, peers = lax.axis_index("lon"), lax.axis_size("lon")
    lon_east, lon_west = lax.rem(lon + 1, peers), lax.rem(lon + peers - 1, peers)
    paired = peers % 2 == 0
    second_of_pair = lax.rem(lon, 2) == 1
    partner = lon + 1 - 2 * lax.rem(lon, 2)

    inputs = [pltpu.make_async_copy(ens.at[:, l, :], field.at[l, :, pad:pad + columns], loads.at[l])
              for l in range(levels)]
    for load in inputs:
        load.start()

    barrier = pltpu.get_barrier_semaphore()
    for side in (lon_east, lon_west):
        pl.semaphore_signal(barrier, inc=1, device_id={"lon": side}, device_id_type=MESH)

    def greet(s, _):
        pl.semaphore_signal(barrier, inc=1, device_id={"mem": lax.rem(me + s, n)}, device_id_type=MESH)
        return 0

    lax.fori_loop(1, n, greet, 0)
    pl.semaphore_wait(barrier, n + 1)

    halo = []
    for l in range(levels):
        for side, (dst, take, put) in enumerate((
                (lon_east, columns - pad, 0), (lon_west, 0, pad + columns))):
            halo.append(pltpu.make_async_remote_copy(
                src_ref=ens.at[:, l, take:take + pad], dst_ref=field.at[l, :, put:put + pad],
                send_sem=edges.at[0, side, l], recv_sem=edges.at[1, side, l],
                device_id={"lon": dst}, device_id_type=MESH))
    for edge in halo:
        edge.start()

    def rows_of(device):
        return pl.ds(pl.multiple_of(device * group, group), group)

    def columns_of(device):
        return pl.ds(pl.multiple_of(device * width, width), width)

    def there(dst, owner):
        return pltpu.make_async_remote_copy(
            src_ref=outbuf.at[:, rows_of(dst), :], dst_ref=slab.at[:, rows_of(owner), :],
            send_sem=send1.at[dst], recv_sem=recv1.at[owner],
            device_id={"mem": dst}, device_id_type=MESH)

    def back(dst, owner):
        return pltpu.make_async_remote_copy(
            src_ref=outbuf.at[:, rows_of(dst), :], dst_ref=backbuf.at[:, rows_of(owner), :],
            send_sem=send2.at[dst], recv_sem=recv2.at[owner],
            device_id={"mem": dst}, device_id_type=MESH)

    def place(owner):
        return [pltpu.make_async_copy(
            backbuf.at[l, rows_of(owner), :], out.at[:, l, columns_of(owner)], stores.at[owner, l])
            for l in range(levels)]

    def advance(dst):
        for l in range(levels):
            value = field[l, :, pl.ds(pl.multiple_of(dst * width, 128), width + 2 * pad)]
            span = width + 2 * pad
            west = pltpu.roll(value, 1, 1)[:, pad:pad + width]
            east = pltpu.roll(value, span - 1, 1)[:, pad:pad + width]
            centre = value[:, pad:pad + width]
            f = flow[l:l + 1, columns_of(dst)]
            outbuf[l, rows_of(dst), :] = (
                centre - jnp.maximum(f, 0.0) * (centre - west) - jnp.minimum(f, 0.0) * (east - centre))

    own = pltpu.make_async_copy(outbuf.at[:, rows_of(me), :], slab.at[:, rows_of(me), :], local.at[0])
    for load in inputs:
        load.wait()

    def send_forecast(dst):
        advance(dst)

        @pl.when(dst != me)
        def _():
            there(dst, me).start()

        @pl.when(dst == me)
        def _():
            own.start()

    if paired:

        @pl.when(second_of_pair)
        def _():
            pl.semaphore_wait(gate, 1)

    def nth(s):
        return jnp.where(s < n - 2, 1 + lax.rem(me + s, n - 2), (s - (n - 2)) * (n - 1))

    def serve(s, _):
        send_forecast(nth(s))
        return 0

    lax.fori_loop(0, n - 2, serve, 0)
    for edge in halo:
        edge.wait()
    lax.fori_loop(n - 2, n, serve, 0)

    def fill(b, _):
        at = pl.ds(pl.multiple_of(b * step, step), step)
        cell = lax.broadcasted_iota(jnp.int32, (step, onehot.shape[1]), 0) + b * step
        onehot[at, :] = jnp.where(cell == cells[...], 1.0, 0.0).astype(bf16)
        return 0

    lax.fori_loop(0, total_cells // step, fill, 0)
    live = lax.broadcasted_iota(jnp.int32, cells.shape, 1) < count[...]
    reach = prec[...] * jnp.exp(-0.5 * (dist[...].astype(f32) / loc_scale) ** 2)
    weights = jnp.where(live, reach, 0.0)

    def sent(s, _):
        dst = nth(s)

        @pl.when(dst != me)
        def _():
            there(dst, me).wait_send()

        return 0

    lax.fori_loop(0, n // 2, sent, 0)
    if paired:

        @pl.when(jnp.logical_not(second_of_pair))
        def _():
            pl.semaphore_signal(gate, inc=1, device_id={"lon": partner}, device_id_type=MESH)

    lax.fori_loop(n // 2, n, sent, 0)

    def block_sum(src):
        at = pl.ds(pl.multiple_of(src * group, group), group)
        return jnp.concatenate(
            [jnp.sum(slab[l, at, :], axis=0, keepdims=True) for l in range(levels)], axis=1)

    own.wait()

    def gather(s, acc):
        src = lax.rem(me + n - s, n)
        there(src, src).wait_recv()
        return acc + block_sum(src)

    mean = lax.fori_loop(1, n, gather, block_sum(me)) / members
    rows[0:1, :] = mean

    picked = jnp.sum(dot(three_rows(mean), onehot[...], ((1,), (0,))), axis=0, keepdims=True)
    forcing = weights * (readings[...] - picked)
    coef = jnp.sum(dot(three_rows(forcing), onehot[...], ((1,), (1,))), axis=0, keepdims=True)

    def centre(b, _):
        at = pl.ds(pl.multiple_of(b * step, step), step)
        drive = jnp.zeros((step, width), f32)
        for l in range(levels):
            part = slice(l * width, (l + 1) * width)
            p = slab[l, at, :] - mean[:, part]
            low[at, part] = p.astype(bf16)
            drive = drive + p * coef[:, part]
        rows[1:2, at] = as_row(jnp.sum(drive, axis=1, keepdims=True))
        o = dot(low[at, :], onehot[...], ((1,), (0,)))
        obs[at, :] = o.astype(bf16)
        wtd[at, :] = (o.astype(bf16).astype(f32) * weights).astype(bf16)
        return 0

    lax.fori_loop(0, blocks, centre, 0)

    def eye(b):
        r = lax.broadcasted_iota(jnp.int32, (step, members), 0) + b * step
        return r == lax.broadcasted_iota(jnp.int32, (step, members), 1)

    def make_gram(b, bound):
        at = pl.ds(pl.multiple_of(b * step, step), step)
        g = dot(obs[at, :], wtd[...], ((1,), (1,))) + jnp.where(eye(b), members - 1.0, 0.0)
        big[at, :] = g
        sums = jnp.sum(jnp.abs(g), axis=1, keepdims=True)
        return jnp.maximum(bound, jnp.max(sums, axis=0, keepdims=True))

    bound = lax.fori_loop(0, blocks, make_gram, jnp.zeros((1, 1), f32))

    def first(b, _):
        at = pl.ds(pl.multiple_of(b * step, step), step)
        scaled = big[at, :] / bound
        poly_a[at, :] = scaled.astype(bf16)
        poly_b[at, :] = (jnp.where(eye(b), 1.5, 0.0) - 0.5 * scaled).astype(bf16)
        return 0

    lax.fori_loop(0, blocks, first, 0)

    def root(b, _):
        at = pl.ds(pl.multiple_of(b * step, step), step)
        poly_c[at, :] = dot(poly_a[at, :], poly_b[...], ((1,), (0,))).astype(bf16)
        return 0

    lax.fori_loop(0, blocks, root, 0)

    def second(b, _):
        at = pl.ds(pl.multiple_of(b * step, step), step)
        product = dot(poly_b[at, :], poly_c[...], ((1,), (0,)))
        s = (jnp.where(eye(b), 1.5, 0.0) - 0.5 * product).astype(bf16)
        inv = dot(s, poly_b[...], ((1,), (0,)))
        big[at, :] = inv
        rows[2:3, at] = as_row(jnp.sum(inv * rows[1:2, :], axis=1, keepdims=True))
        return 0

    lax.fori_loop(0, blocks, second, 0)
    stretch = jnp.sqrt((members - 1.0) / bound)

    def transform(b, _):
        at = pl.ds(pl.multiple_of(b * step, step), step)
        inv = big[at, :]
        weight = jnp.sum(inv * rows[2:3, :], axis=1, keepdims=True) / bound
        poly_a[at, :] = (weight + stretch * inv).astype(bf16)
        return 0

    lax.fori_loop(0, blocks, transform, 0)

    tile = max(128, group)
    tiles = members // tile
    each = tile // group

    def apply(t, _):
        b = lax.rem(me // each + 1 + t, tiles)
        at = pl.ds(pl.multiple_of(b * tile, tile), tile)
        value = dot(poly_a[:, at], low[...], ((0,), (0,))) + rows[0:1, :]
        for l in range(levels):
            outbuf[l, at, :] = value[:, l * width:(l + 1) * width]
        for g in range(each):
            dst = b * each + g

            @pl.when(dst != me)
            def _():
                back(dst, me).start()
        return 0

    lax.fori_loop(0, tiles, apply, 0)
    backbuf[:, rows_of(me), :] = outbuf[:, rows_of(me), :]
    for put in place(me):
        put.start()

    def arrive(s, _):
        src = lax.rem(me + n - s, n)
        back(src, src).wait_recv()
        for put in place(src):
            put.start()
        return 0

    lax.fori_loop(1, n, arrive, 0)

    def finish(s, _):
        dst = lax.rem(me + n - s, n)
        back(dst, me).wait_send()
        for put in place(dst):
            put.wait()
        return 0

    lax.fori_loop(1, n, finish, 0)
    for put in place(me):
        put.wait()


def per_device(ensemble, flow, obs_index, obs_count, obs_dist, readings, prec):
    n = lax.axis_size("mem")
    group, levels, columns = ensemble.shape
    members, width = group * n, columns // n
    cells, slots = levels * width, obs_index.shape[1]
    vmem = pl.BlockSpec(memory_space=pltpu.VMEM)
    hbm = pl.BlockSpec(memory_space=pl.ANY)
    slab = pltpu.VMEM((levels, members, width), f32)
    square = pltpu.VMEM((members, members), bf16)
    return pl.pallas_call(
        functools.partial(kernel, n),
        out_shape=jax.ShapeDtypeStruct(ensemble.shape, f32),
        in_specs=[hbm] + [vmem] * 6,
        out_specs=hbm,
        scratch_shapes=[
            pltpu.VMEM((levels, group, columns + 256), f32),
            slab,
            pltpu.VMEM((members, cells), bf16),
            pltpu.VMEM((cells, slots), bf16),
            pltpu.VMEM((members, slots), bf16),
            pltpu.VMEM((members, slots), bf16),
            pltpu.VMEM((members, members), f32),
            square,
            square,
            square,
            pltpu.VMEM((8, max(members, cells)), f32),
            slab,
            slab,
            pltpu.SemaphoreType.DMA((2, 2, levels)),
            pltpu.SemaphoreType.DMA((levels,)),
            pltpu.SemaphoreType.DMA((n, levels)),
            pltpu.SemaphoreType.DMA((n,)),
            pltpu.SemaphoreType.DMA((n,)),
            pltpu.SemaphoreType.DMA((n,)),
            pltpu.SemaphoreType.DMA((n,)),
            pltpu.SemaphoreType.DMA((1,)),
            pltpu.SemaphoreType.REGULAR,
        ],
        compiler_params=pltpu.CompilerParams(
            collective_id=0, has_side_effects=True, vmem_limit_bytes=60 * 1024 * 1024),
        name="regroup_analyse",
    )(ensemble, flow, obs_index, obs_count[:, None], obs_dist, prec, readings)


def solution(mesh):
    placed = (
        P("mem", None, "lon"),
        P(None, "lon"),
        P(("mem", "lon"), None),
        P(("mem", "lon")),
        P(("mem", "lon"), None),
        P(("mem", "lon"), None),
        P(("mem", "lon"), None),
    )
    return jax.shard_map(
        per_device, mesh=mesh, in_specs=placed, out_specs=P("mem", None, "lon"), check_vma=False
    )
```

```python
import functools
import jax
import jax.numpy as jnp
from jax import lax
from jax.experimental import pallas as pl
from jax.experimental.pallas import tpu as pltpu
from jax.sharding import PartitionSpec as P

loc_scale = 12.0
MESH = pl.DeviceIdType.MESH
f32, bf16 = jnp.float32, jnp.bfloat16


def dot(a, b, dims):
    return lax.dot_general(a, b, (dims, ((), ())), preferred_element_type=f32)


def three_rows(row):
    hi = row.astype(bf16).astype(f32)
    mid = (row - hi).astype(bf16).astype(f32)
    low = row - hi - mid
    which = lax.broadcasted_iota(jnp.int32, (16, row.shape[1]), 0)
    rows = jnp.where(which == 0, hi, jnp.where(which == 1, mid, jnp.where(which == 2, low, 0.0)))
    return rows.astype(bf16)


def as_row(column):
    wide = jnp.broadcast_to(column, (column.shape[0], 128))
    return wide.T[0:1, :]


def kernel(n, ens, flow, cells, count, dist, prec, readings, out, field, slab, low, onehot, obs, wtd, big,
           poly_a, poly_b, poly_c, rows, outbuf, backbuf, edges, loads, stores, send1, recv1, send2, recv2,
           local, gate):
    levels, members, width = slab.shape
    group = members // n
    columns = n * width
    pad = 128
    me = lax.axis_index("mem")
    total_cells = levels * width
    step = 256
    blocks = members // step
    lon, peers = lax.axis_index("lon"), lax.axis_size("lon")
    lon_east, lon_west = lax.rem(lon + 1, peers), lax.rem(lon + peers - 1, peers)
    paired = peers % 2 == 0
    second_of_pair = lax.rem(lon, 2) == 1
    partner = lon + 1 - 2 * lax.rem(lon, 2)

    inputs = [pltpu.make_async_copy(ens.at[:, l, :], field.at[l, :, pad:pad + columns], loads.at[l])
              for l in range(levels)]
    for load in inputs:
        load.start()

    barrier = pltpu.get_barrier_semaphore()
    for side in (lon_east, lon_west):
        pl.semaphore_signal(barrier, inc=1, device_id={"lon": side}, device_id_type=MESH)

    def greet(s, _):
        pl.semaphore_signal(barrier, inc=1, device_id={"mem": lax.rem(me + s, n)}, device_id_type=MESH)
        return 0

    lax.fori_loop(1, n, greet, 0)
    pl.semaphore_wait(barrier, n + 1)

    halo = []
    for l in range(levels):
        for side, (dst, take, put) in enumerate((
                (lon_east, columns - pad, 0), (lon_west, 0, pad + columns))):
            halo.append(pltpu.make_async_remote_copy(
                src_ref=ens.at[:, l, take:take + pad], dst_ref=field.at[l, :, put:put + pad],
                send_sem=edges.at[0, side, l], recv_sem=edges.at[1, side, l],
                device_id={"lon": dst}, device_id_type=MESH))
    for edge in halo:
        edge.start()

    def rows_of(device):
        return pl.ds(pl.multiple_of(device * group, group), group)

    def columns_of(device):
        return pl.ds(pl.multiple_of(device * width, width), width)

    def there(dst, owner):
        return pltpu.make_async_remote_copy(
            src_ref=outbuf.at[:, rows_of(dst), :], dst_ref=slab.at[:, rows_of(owner), :],
            send_sem=send1.at[dst], recv_sem=recv1.at[owner],
            device_id={"mem": dst}, device_id_type=MESH)

    def back(dst, owner):
        return pltpu.make_async_remote_copy(
            src_ref=outbuf.at[:, rows_of(dst), :], dst_ref=backbuf.at[:, rows_of(owner), :],
            send_sem=send2.at[dst], recv_sem=recv2.at[owner],
            device_id={"mem": dst}, device_id_type=MESH)

    def place(owner):
        return [pltpu.make_async_copy(
            backbuf.at[l, rows_of(owner), :], out.at[:, l, columns_of(owner)], stores.at[owner, l])
            for l in range(levels)]

    def advance(dst):
        for l in range(levels):
            value = field[l, :, pl.ds(pl.multiple_of(dst * width, 128), width + 2 * pad)]
            span = width + 2 * pad
            west = pltpu.roll(value, 1, 1)[:, pad:pad + width]
            east = pltpu.roll(value, span - 1, 1)[:, pad:pad + width]
            centre = value[:, pad:pad + width]
            f = flow[l:l + 1, columns_of(dst)]
            outbuf[l, rows_of(dst), :] = (
                centre - jnp.maximum(f, 0.0) * (centre - west) - jnp.minimum(f, 0.0) * (east - centre))

    own = pltpu.make_async_copy(outbuf.at[:, rows_of(me), :], slab.at[:, rows_of(me), :], local.at[0])
    for load in inputs:
        load.wait()

    def send_forecast(dst):
        advance(dst)

        @pl.when(dst != me)
        def _():
            there(dst, me).start()

        @pl.when(dst == me)
        def _():
            own.start()

    if paired:

        @pl.when(second_of_pair)
        def _():
            pl.semaphore_wait(gate, 1)

    def nth(s):
        return jnp.where(s < n - 2, 1 + lax.rem(me + s, n - 2), (s - (n - 2)) * (n - 1))

    def serve(s, _):
        send_forecast(nth(s))
        return 0

    lax.fori_loop(0, n - 2, serve, 0)
    for edge in halo:
        edge.wait()
    lax.fori_loop(n - 2, n, serve, 0)

    def fill(b, _):
        at = pl.ds(pl.multiple_of(b * step, step), step)
        cell = lax.broadcasted_iota(jnp.int32, (step, onehot.shape[1]), 0) + b * step
        onehot[at, :] = jnp.where(cell == cells[...], 1.0, 0.0).astype(bf16)
        return 0

    lax.fori_loop(0, total_cells // step, fill, 0)
    live = lax.broadcasted_iota(jnp.int32, cells.shape, 1) < count[...]
    reach = prec[...] * jnp.exp(-0.5 * (dist[...].astype(f32) / loc_scale) ** 2)
    weights = jnp.where(live, reach, 0.0)

    def sent(s, _):
        dst = nth(s)

        @pl.when(dst != me)
        def _():
            there(dst, me).wait_send()

        return 0

    lax.fori_loop(0, n // 2, sent, 0)
    if paired:

        @pl.when(jnp.logical_not(second_of_pair))
        def _():
            pl.semaphore_signal(gate, inc=1, device_id={"lon": partner}, device_id_type=MESH)

    lax.fori_loop(n // 2, n, sent, 0)

    def block_sum(src):
        at = pl.ds(pl.multiple_of(src * group, group), group)
        return jnp.concatenate(
            [jnp.sum(slab[l, at, :], axis=0, keepdims=True) for l in range(levels)], axis=1)

    own.wait()

    def gather(s, acc):
        src = lax.rem(me + n - s, n)
        there(src, src).wait_recv()
        return acc + block_sum(src)

    mean = lax.fori_loop(1, n, gather, block_sum(me)) / members
    rows[0:1, :] = mean

    picked = jnp.sum(dot(three_rows(mean), onehot[...], ((1,), (0,))), axis=0, keepdims=True)
    forcing = weights * (readings[...] - picked)
    coef = jnp.sum(dot(three_rows(forcing), onehot[...], ((1,), (1,))), axis=0, keepdims=True)

    def centre(b, _):
        at = pl.ds(pl.multiple_of(b * step, step), step)
        drive = jnp.zeros((step, width), f32)
        for l in range(levels):
            part = slice(l * width, (l + 1) * width)
            p = slab[l, at, :] - mean[:, part]
            low[at, part] = p.astype(bf16)
            drive = drive + p * coef[:, part]
        rows[1:2, at] = as_row(jnp.sum(drive, axis=1, keepdims=True))
        o = dot(low[at, :], onehot[...], ((1,), (0,)))
        obs[at, :] = o.astype(bf16)
        wtd[at, :] = (o.astype(bf16).astype(f32) * weights).astype(bf16)
        return 0

    lax.fori_loop(0, blocks, centre, 0)

    def eye(b):
        r = lax.broadcasted_iota(jnp.int32, (step, members), 0) + b * step
        return r == lax.broadcasted_iota(jnp.int32, (step, members), 1)

    def make_gram(b, bound):
        at = pl.ds(pl.multiple_of(b * step, step), step)
        g = dot(obs[at, :], wtd[...], ((1,), (1,))) + jnp.where(eye(b), members - 1.0, 0.0)
        big[at, :] = g
        sums = jnp.sum(jnp.abs(g), axis=1, keepdims=True)
        return jnp.maximum(bound, jnp.max(sums, axis=0, keepdims=True))

    bound = lax.fori_loop(0, blocks, make_gram, jnp.zeros((1, 1), f32))

    def first(b, _):
        at = pl.ds(pl.multiple_of(b * step, step), step)
        scaled = big[at, :] / bound
        poly_a[at, :] = scaled.astype(bf16)
        poly_b[at, :] = (jnp.where(eye(b), 1.5, 0.0) - 0.5 * scaled).astype(bf16)
        return 0

    lax.fori_loop(0, blocks, first, 0)

    def root(b, _):
        at = pl.ds(pl.multiple_of(b * step, step), step)
        poly_c[at, :] = dot(poly_a[at, :], poly_b[...], ((1,), (0,))).astype(bf16)
        return 0

    lax.fori_loop(0, blocks, root, 0)

    def second(b, _):
        at = pl.ds(pl.multiple_of(b * step, step), step)
        product = dot(poly_b[at, :], poly_c[...], ((1,), (0,)))
        s = (jnp.where(eye(b), 1.5, 0.0) - 0.5 * product).astype(bf16)
        inv = dot(s, poly_b[...], ((1,), (0,)))
        big[at, :] = inv
        rows[2:3, at] = as_row(jnp.sum(inv * rows[1:2, :], axis=1, keepdims=True))
        return 0

    lax.fori_loop(0, blocks, second, 0)
    stretch = jnp.sqrt((members - 1.0) / bound)

    def transform(b, _):
        at = pl.ds(pl.multiple_of(b * step, step), step)
        inv = big[at, :]
        weight = jnp.sum(inv * rows[2:3, :], axis=1, keepdims=True) / bound
        poly_a[at, :] = (weight + stretch * inv).astype(bf16)
        return 0

    lax.fori_loop(0, blocks, transform, 0)

    tile = max(128, group)
    tiles = members // tile
    each = tile // group

    def apply(t, _):
        b = lax.rem(me // each + 1 + t, tiles)
        at = pl.ds(pl.multiple_of(b * tile, tile), tile)
        value = dot(poly_a[:, at], low[...], ((0,), (0,))) + rows[0:1, :]
        for l in range(levels):
            outbuf[l, at, :] = value[:, l * width:(l + 1) * width]
        for g in range(each):
            dst = b * each + g

            @pl.when(dst != me)
            def _():
                back(dst, me).start()
        return 0

    lax.fori_loop(0, tiles, apply, 0)
    backbuf[:, rows_of(me), :] = outbuf[:, rows_of(me), :]
    for put in place(me):
        put.start()

    def arrive(s, _):
        src = lax.rem(me + n - s, n)
        back(src, src).wait_recv()
        for put in place(src):
            put.start()
        return 0

    lax.fori_loop(1, n, arrive, 0)

    def finish(s, _):
        dst = lax.rem(me + n - s, n)
        back(dst, me).wait_send()
        for put in place(dst):
            put.wait()
        return 0

    lax.fori_loop(1, n, finish, 0)
    for put in place(me):
        put.wait()


def per_device(ensemble, flow, obs_index, obs_count, obs_dist, readings, prec):
    n = lax.axis_size("mem")
    group, levels, columns = ensemble.shape
    members, width = group * n, columns // n
    cells, slots = levels * width, obs_index.shape[1]
    vmem = pl.BlockSpec(memory_space=pltpu.VMEM)
    hbm = pl.BlockSpec(memory_space=pl.ANY)
    slab = pltpu.VMEM((levels, members, width), f32)
    square = pltpu.VMEM((members, members), bf16)
    return pl.pallas_call(
        functools.partial(kernel, n),
        out_shape=pltpu.VMEM(ensemble.shape, f32),
        in_specs=[hbm] + [vmem] * 6,
        out_specs=vmem,
        scratch_shapes=[
            pltpu.VMEM((levels, group, columns + 256), f32),
            slab,
            pltpu.VMEM((members, cells), bf16),
            pltpu.VMEM((cells, slots), bf16),
            pltpu.VMEM((members, slots), bf16),
            pltpu.VMEM((members, slots), bf16),
            pltpu.VMEM((members, members), f32),
            square,
            square,
            square,
            pltpu.VMEM((8, max(members, cells)), f32),
            slab,
            slab,
            pltpu.SemaphoreType.DMA((2, 2, levels)),
            pltpu.SemaphoreType.DMA((levels,)),
            pltpu.SemaphoreType.DMA((n, levels)),
            pltpu.SemaphoreType.DMA((n,)),
            pltpu.SemaphoreType.DMA((n,)),
            pltpu.SemaphoreType.DMA((n,)),
            pltpu.SemaphoreType.DMA((n,)),
            pltpu.SemaphoreType.DMA((1,)),
            pltpu.SemaphoreType.REGULAR,
        ],
        compiler_params=pltpu.CompilerParams(
            collective_id=0, has_side_effects=True, vmem_limit_bytes=67043328 - 4 * ensemble.size - 4096),
        name="regroup_analyse",
    )(ensemble, flow, obs_index, obs_count[:, None], obs_dist, prec, readings)


def solution(mesh):
    placed = (
        P("mem", None, "lon"),
        P(None, "lon"),
        P(("mem", "lon"), None),
        P(("mem", "lon")),
        P(("mem", "lon"), None),
        P(("mem", "lon"), None),
        P(("mem", "lon"), None),
    )
    return jax.shard_map(
        per_device, mesh=mesh, in_specs=placed, out_specs=P("mem", None, "lon"), check_vma=False
    )
```
